256 devices in a mesh: dom: 128 (over x, y_lo, z, core), feat: 2 (over y_hi).
Axes of the slice: x: 4, y: 4 (y_hi: 2, y_lo: 2; y = y_hi * 2 + y_lo), z: 8, core: 2. Of those that a mesh axis runs over, the one named last changes fastest.
Arguments:
- features: float32 [262144, 512], P('dom', 'feat'), may hold values from -6 to 6
- infill_mask: int32 [262144], P('dom'), may hold values 0 or 1
- mask_token: float32 [512], P('feat'), may hold values from -4 to 4
- local_rows: int32 [128, 64], P('dom'), may hold values from 0 to 15
- local_cols: int32 [128, 64], P('dom'), may hold values from 12 to 35, as said below
- local_tiles: float32 [128, 64, 128, 128], P('dom'), may hold values from -0.1875 to 0.1875
- hub_ids: int32 [4096], P('dom'), may hold values from 0 to 262143, as said below
- hub_count: int32 [128], P('dom'), may hold values from 16 to 64, as said below
- hub_rows: int32 [128, 64], P('dom'), may hold values from 0 to 15
- hub_panels: int32 [128, 64], P('dom'), may hold values from 0 to 31
- hub_tiles: float32 [128, 64, 128, 128], P('dom'), may hold values from -0.1875 to 0.1875
- mix_weight: float32 [512, 512], P(None, 'feat'), may hold values from -0.25 to 0.25
- mix_bias: float32 [512], P('feat'), may hold values from -3 to 3
- norm_gain: float32 [512], P('feat'), may hold values from 0.25 to 1.75
Outputs:
- updated: float32 [262144, 512], P('dom', 'feat')
The draws below stay inside these ranges and needn't reach their ends.
Inputs may be any that keep to these rules, and one draw needn't show every extreme that they name: `hub_ids`: index block k of 32 entries holds distinct vertices of partition k. `hub_count`: some partition has all 64 slots live. `local_cols`: each local tile's column block differs from its row block plus 2048 // 128 by at most 4, and in every partition by exactly 4 on both sides.
All inputs are finite; a program needn't handle non-finite values. No bound on the sum of `infill_mask` on one device may be relied on, other than what follows from the above.
Results may differ from the reference program's by a relative error of at most 0.0003.
Values sent between devices are 32-bit elements; how exact they have to be, the bound alone decides.
No kernel may reach another device: no remote copies, remote signals or barrier semaphores. Data moves between devices by JAX's collectives and lax.ppermute only.
A program may use at most 128 MiB of HBM per device.

```python
import jax
import jax.numpy as jnp
from jax import lax

D = 512
ROWS = 2048
LOC_TILES = 64
HUB_TILES = 64
HUB_DEV = 32
REACH = 4
VERTICES = 262144
HUBS = 4096
N_DOM = 128


def local_layout(key):
    blocks = ROWS // 128
    rows_key = jax.random.fold_in(key, 31)
    offs_key = jax.random.fold_in(key, 32)
    row_blocks = jax.random.randint(rows_key, (N_DOM, LOC_TILES), 0, blocks)
    offsets = jax.random.randint(offs_key, (N_DOM, LOC_TILES), -REACH, REACH + 1)
    row_blocks = row_blocks.at[:, 0].set(0).at[:, 1].set(blocks - 1)
    offsets = offsets.at[:, 0].set(-REACH).at[:, 1].set(REACH)
    columns = row_blocks + blocks + offsets
    return (row_blocks.astype(jnp.int32), columns.astype(jnp.int32))


def draw_local_rows(key, part):
    return local_layout(key)[0]


def draw_local_cols(key, part):
    return local_layout(key)[1]


def draw_hub_ids(key, part):

    def owner_ids(owner):
        order = jax.random.permutation(jax.random.fold_in(key, owner), ROWS)[:HUB_DEV]
        return order.astype(jnp.int32) + owner * ROWS
    return jax.vmap(owner_ids)(jnp.arange(N_DOM, dtype=jnp.int32)).reshape(-1)


def draw_hub_count(key, part):
    counts = jax.random.randint(jax.random.fold_in(key, 11), (N_DOM,), HUB_TILES // 4, HUB_TILES + 1)
    fullest = jax.random.randint(jax.random.fold_in(key, 12), (), 0, N_DOM)
    return counts.at[fullest].set(HUB_TILES).astype(jnp.int32)


def set_ends(drawn, rng, least, top_value):
    index_at = [jax.random.randint(jax.random.fold_in(rng, axis), (), 0, length) for axis, length in enumerate(drawn.shape)]
    widest = drawn.shape.index(max(drawn.shape))
    next_to = index_at[:widest] + [(index_at[widest] + 1) % drawn.shape[widest]] + index_at[widest + 1:]
    return drawn.at[tuple(index_at)].set(least).at[tuple(next_to)].set(top_value)


def block_scale(stream_key, extent, pieces, least, largest):
    factor_of, own = 1.0, jax.random.fold_in(stream_key, 6)
    for dim, parts in pieces:
        heights = jnp.exp(jax.random.uniform(jax.random.fold_in(own, dim), (parts,), jnp.float32, least / len(pieces), largest / len(pieces)))
        factor_of = factor_of * jnp.repeat(heights, extent[dim] // parts).reshape([-1 if axis == dim else 1 for axis in range(len(extent))])
    return factor_of


def bell_draw(rng, dims, scale, reach, shards=(), held_as=jnp.bfloat16):
    values = scale * jax.random.normal(rng, dims, jnp.float32)
    if shards:
        values = values * block_scale(rng, dims, shards, -0.22, 0.18)
    return jnp.clip(values, -reach, reach).astype(held_as)


def setup_inputs(seed: int = 0) -> dict:
    key_of = jax.random.split(jax.random.key(seed), 15)
    return {
        "features": bell_draw(key_of[0], (VERTICES, D), 1.0, 6.0, ((0, 128), (1, 2)), jnp.float32),
        "infill_mask": set_ends((jax.random.randint(key_of[1], (VERTICES,), 0, 20) < 3).astype(jnp.int32), jax.random.fold_in(key_of[1], 1), 0, 1),
        "mask_token": bell_draw(key_of[2], (D,), 1.0, 4.0, ((0, 2),), jnp.float32),
        "local_rows": draw_local_rows(jax.random.fold_in(key_of[14], 71), 0),
        "local_cols": draw_local_cols(jax.random.fold_in(key_of[14], 71), 0),
        "local_tiles": bell_draw(key_of[5], (N_DOM, LOC_TILES, 128, 128), 1024 ** -0.5, 0.1875, ((0, 128),), jnp.float32),
        "hub_ids": draw_hub_ids(jax.random.fold_in(key_of[14], 71), 0),
        "hub_count": draw_hub_count(jax.random.fold_in(key_of[14], 71), 0),
        "hub_rows": set_ends(jax.random.randint(key_of[8], (N_DOM, HUB_TILES), 0, ROWS // 128), jax.random.fold_in(key_of[8], 1), 0, (ROWS // 128) - 1).astype(jnp.int32),
        "hub_panels": set_ends(jax.random.randint(key_of[9], (N_DOM, HUB_TILES), 0, HUBS // 128), jax.random.fold_in(key_of[9], 1), 0, (HUBS // 128) - 1).astype(jnp.int32),
        "hub_tiles": bell_draw(key_of[10], (N_DOM, HUB_TILES, 128, 128), 1024 ** -0.5, 0.1875, ((0, 128),), jnp.float32),
        "mix_weight": bell_draw(key_of[11], (D, D), D ** -0.5, 0.25, ((1, 2),), jnp.float32),
        "mix_bias": bell_draw(key_of[12], (D,), 0.5, 3.0, ((0, 2),), jnp.float32),
        "norm_gain": jnp.clip(1.0 + 0.15 * jax.random.normal(key_of[13], (D,), jnp.float32), 0.25, 1.75),
    }


def reference(features, infill_mask, mask_token, local_rows, local_cols, local_tiles, hub_ids, hub_count, hub_rows, hub_panels, hub_tiles, mix_weight, mix_bias, norm_gain):
    highest = lax.Precision.HIGHEST
    filled = jnp.where(infill_mask[:, None] == 1, mask_token[None, :], features)
    empty = jnp.zeros((ROWS, D), jnp.float32)
    padded = jnp.concatenate([empty, filled, empty], 0)
    panels = filled[hub_ids].reshape(HUBS // 128, 128, D)
    blocks = ROWS // 128
    block_ids = jnp.arange(blocks, dtype=jnp.int32)

    def partition(index):
        extended = lax.dynamic_slice_in_dim(padded, (index * ROWS).astype(jnp.int32), 3 * ROWS, 0)
        ext_blocks = extended.reshape(3 * blocks, 128, D)
        picked = ext_blocks[local_cols[index]]
        products = jnp.einsum('tij,tjf->tif', local_tiles[index], picked, precision=highest)
        row_onehot = (local_rows[index][None, :] == block_ids[:, None]).astype(jnp.float32)
        total = jnp.einsum('rt,tif->rif', row_onehot, products, precision=highest)
        hub_picked = panels[hub_panels[index]]
        hub_products = jnp.einsum('tij,tjf->tif', hub_tiles[index], hub_picked, precision=highest)
        live = (jnp.arange(HUB_TILES, dtype=jnp.int32) < hub_count[index]).astype(jnp.float32)
        hub_onehot = (hub_rows[index][None, :] == block_ids[:, None]).astype(jnp.float32) * live[None, :]
        total = total + jnp.einsum('rt,tif->rif', hub_onehot, hub_products, precision=highest)
        aggregate = total.reshape(ROWS, D)
        own = lax.dynamic_slice_in_dim(filled, (index * ROWS).astype(jnp.int32), ROWS, 0)
        pre = jnp.dot(aggregate, mix_weight, precision=highest) + mix_bias[None, :]
        hidden = own + jax.nn.silu(pre)
        mean_val = lax.optimization_barrier(jnp.sum(hidden, 1, keepdims=True)) / D
        square_val = lax.optimization_barrier(jnp.sum(hidden * hidden, 1, keepdims=True)) / D
        scale_val = lax.rsqrt(square_val - mean_val * mean_val + 1e-05)
        return (hidden - mean_val) * scale_val * norm_gain[None, :]
    result = lax.map(partition, jnp.arange(N_DOM, dtype=jnp.int32))
    return result.reshape(VERTICES, D)
```

```python
import jax
import jax.numpy as jnp
from jax import lax
from jax.experimental import pallas as pl
from jax.experimental.pallas import tpu as pltpu
from jax.sharding import PartitionSpec as P

NX, NYL, NZ, NC = 4, 2, 8, 2
BOTH = ("dom", "feat")
F32 = jnp.float32
BF = jnp.bfloat16
SMEM = pl.BlockSpec(memory_space=pltpu.SMEM)
VMEM = pl.BlockSpec(memory_space=pltpu.VMEM)
ANY = pl.BlockSpec(memory_space=pl.ANY)


def dom_index(x, yl, z, c):
    return ((x * NYL + yl) * NZ + z) * NC + c


def shift(move):
    pairs = []
    for x in range(NX):
        for yl in range(NYL):
            for z in range(NZ):
                for c in range(NC):
                    for f in range(2):
                        tx, tyl, tz, tc, tf = move(x, yl, z, c, f)
                        pairs.append(
                            (
                                dom_index(x, yl, z, c) * 2 + f,
                                dom_index(tx % NX, tyl, tz % NZ, tc) * 2 + tf,
                            )
                        )
    return pairs


def send(value, move):
    return lax.ppermute(value, BOTH, shift(move))


def place():
    dom = lax.axis_index("dom")
    c = dom % NC
    z = (dom // NC) % NZ
    yl = (dom // (NC * NZ)) % NYL
    x = dom // (NC * NZ * NYL)
    return x, yl, z, c


def split(a):
    hi = a.astype(BF)
    return hi, (a - hi.astype(F32)).astype(BF)


def dot(a, b):
    return jnp.dot(a, b, preferred_element_type=F32)


def hub_rows_kernel(ids, mask, features, token, out, sems):
    first = lax.axis_index("dom") * features.shape[0]
    count = out.shape[0]
    copies = []
    for i in range(count):
        row = ids[i] - first
        copies.append(
            pltpu.make_async_copy(features.at[pl.ds(row, 1)], out.at[pl.ds(i, 1)], sems.at[i])
        )
        copies[-1].start()
    for i in range(count):
        copies[i].wait()
    for i in range(count):
        row = ids[i] - first

        @pl.when(mask[row] == 1)
        def _():
            out[pl.ds(i, 1), :] = token[...]


def hub_rows_of(hub_ids, infill_mask, features, mask_token):
    count = hub_ids.shape[0]
    return pl.pallas_call(
        hub_rows_kernel,
        out_shape=jax.ShapeDtypeStruct((count, features.shape[1]), F32),
        in_specs=[SMEM, SMEM, ANY, VMEM],
        out_specs=VMEM,
        scratch_shapes=[pltpu.SemaphoreType.DMA((count,))],
        name="hub_rows",
    )(hub_ids, infill_mask, features, mask_token[None, :])


def mix_rows(xf, xg, weight):
    f = lax.axis_index("feat")
    half = xf.shape[1]
    wf = weight[pl.ds(pl.multiple_of(f * half, half), half), :]
    wg = weight[pl.ds(pl.multiple_of((1 - f) * half, half), half), :]
    wfh, wfl = split(wf)
    wgh, wgl = split(wg)
    right = jnp.concatenate([wfh, wfl, wfh, wgh, wgl, wgh], 0)
    fh, fl = split(xf)
    gh, gl = split(xg)
    left = jnp.concatenate([fh, fh, fl, gh, gh, gl], 1)
    return dot(left, right)


def mix_kernel(xf, xg, weight, out):
    step = 256
    for i in range(xf.shape[0] // step):
        at = pl.ds(i * step, step)
        out[at, :] = mix_rows(xf[at, :], xg[at, :], weight)


def mix(xf, xg, weight):
    rows, half = xf.shape
    return pl.pallas_call(
        mix_kernel,
        out_shape=jax.ShapeDtypeStruct((rows, half), F32),
        in_specs=[VMEM] * 3,
        out_specs=VMEM,
        name="mix_rows",
        cost_estimate=pl.CostEstimate(
            flops=rows * half * half * 12, bytes_accessed=rows * half * 12, transcendentals=0
        ),
        compiler_params=pltpu.CompilerParams(vmem_limit_bytes=16 << 20),
    )(xf, xg, weight)


def mix_hub_kernel(own_f, own_g, other_f, other_g, weight, out):
    count = own_f.shape[0]
    yl = place()[1]
    xf = jnp.concatenate([own_f[...], other_f[...]], 0)
    xg = jnp.concatenate([own_g[...], other_g[...]], 0)
    y = mix_rows(xf, xg, weight)
    out[pl.ds(pl.multiple_of(yl * count, count), count), :] = y[:count]
    out[pl.ds(pl.multiple_of((1 - yl) * count, count), count), :] = y[count:]


def mix_hub(own_f, own_g, other_f, other_g, weight):
    count, half = own_f.shape
    return pl.pallas_call(
        mix_hub_kernel,
        out_shape=jax.ShapeDtypeStruct((2 * count, half), F32),
        in_specs=[VMEM] * 5,
        out_specs=VMEM,
        name="mix_hub",
    )(own_f, own_g, other_f, other_g, weight)


def tile_product(tile, y):
    ah, al = split(tile)
    yh, yl = split(y)
    return dot(jnp.concatenate([ah, ah, al], 1), jnp.concatenate([yh, yl, yh], 0))


UNROLL = 8


def local_kernel(rows, cols, tiles, prev, first, mid, last, after, total, ext):
    total[...] = jnp.zeros_like(total)
    at = 0
    for part in (prev, first, mid, last, after):
        n = part.shape[0] // 128
        ext[pl.ds(at, n)] = part[...].reshape(n, 128, part.shape[1])
        at += n
    low = total.shape[0] - (ext.shape[0] - total.shape[0]) // 2

    def step(i, carry):
        products = []
        for u in range(UNROLL):
            t = i * UNROLL + u
            products.append(tile_product(tiles[t], ext[cols[0, t] - low]))
        for u in range(UNROLL):
            total[rows[0, i * UNROLL + u]] += products[u]
        return carry

    lax.fori_loop(0, tiles.shape[0] // UNROLL, step, 0)


def local_sum(rows, cols, tiles, parts, blocks):
    half = parts[0].shape[1]
    depth = sum(p.shape[0] for p in parts) // 128
    count = tiles.shape[0]
    return pl.pallas_call(
        local_kernel,
        out_shape=jax.ShapeDtypeStruct((blocks, 128, half), F32),
        in_specs=[SMEM, SMEM] + [VMEM] * 6,
        out_specs=VMEM,
        scratch_shapes=[pltpu.VMEM((depth, 128, half), F32)],
        name="local_tiles",
        cost_estimate=pl.CostEstimate(
            flops=count * 128 * 128 * half * 6, bytes_accessed=12 << 20, transcendentals=0
        ),
        compiler_params=pltpu.CompilerParams(vmem_limit_bytes=24 << 20),
    )(rows, cols, tiles, *parts)


def hub_kernel(
    count_ref, rows, panels, tiles, total_in, filled, bias, *rest
):
    parts = rest[: 2 * NX]
    hidden, stats, total, held, sems = rest[2 * NX :]
    copies = []
    for side in range(2):
        for dx in range(NX):
            copies.append(
                pltpu.make_async_copy(
                    parts[side * NX + dx], held.at[side, dx], sems.at[side * NX + dx]
                )
            )
            copies[-1].start()
    total[...] = total_in[...]
    for copy in copies:
        copy.wait()
    x, yl, z, c = place()
    live = count_ref[0]
    hubs = held.shape[3] // NYL

    def panel(p):
        px = p // 8
        pyl = (p // 4) % 2
        dx = (x - px + NX) % NX
        slabs = []
        for k in range(4):
            pz = 2 * (p % 4) + k // 2
            dz = (z - pz + NZ) % NZ
            side = (c + k % 2) % 2
            slabs.append(held[side, dx, dz, pl.ds(pl.multiple_of(pyl * hubs, hubs), hubs), :])
        return jnp.concatenate(slabs, 0)

    def step(i, carry):
        products = []
        for u in range(UNROLL):
            t = i * UNROLL + u
            product = tile_product(tiles[t], panel(panels[0, t]))
            products.append(jnp.where(t < live, product, 0.0))
        for u in range(UNROLL):
            total[rows[0, i * UNROLL + u]] += products[u]
        return carry

    lax.fori_loop(0, (live + UNROLL - 1) // UNROLL, step, 0)

    blocks = total.shape[0]
    for b in range(blocks):
        at = pl.ds(b * 128, 128)
        v = total[b] + bias[...]
        h = filled[at, :] + v / (1.0 + jnp.exp(-v))
        hidden[at, :] = h
        q = h * h
        s = h[:, :128] + h[:, 128:]
        q = q[:, :128] + q[:, 128:]
        stats[pl.ds(b, 1), :] = jnp.sum(s.T, 0, keepdims=True)
        stats[pl.ds(blocks + b, 1), :] = jnp.sum(q.T, 0, keepdims=True)


def hub_and_hidden(count, rows, panels, tiles, total, filled, bias, parts):
    blocks, _, half = total.shape
    n = filled.shape[0]
    return pl.pallas_call(
        hub_kernel,
        out_shape=[
            jax.ShapeDtypeStruct((n, half), F32),
            jax.ShapeDtypeStruct((2 * blocks, 128), F32),
        ],
        in_specs=[SMEM, SMEM, SMEM, VMEM, VMEM, VMEM, VMEM] + [ANY] * (2 * NX),
        out_specs=[VMEM, VMEM],
        scratch_shapes=[
            pltpu.VMEM((blocks, 128, half), F32),
            pltpu.VMEM((2, NX) + parts[0].shape, F32),
            pltpu.SemaphoreType.DMA((2 * NX,)),
        ],
        name="hub_tiles",
        cost_estimate=pl.CostEstimate(
            flops=tiles.shape[0] * 128 * 128 * half * 6, bytes_accessed=16 << 20, transcendentals=0
        ),
        compiler_params=pltpu.CompilerParams(vmem_limit_bytes=32 << 20),
    )(count, rows, panels, tiles, total, filled, bias[None, :], *parts)


def norm_kernel(width, hidden, own, other, gain, out):
    blocks = own.shape[0] // 2
    sums = (own[...] + other[...]) / width
    for b in range(blocks):
        mean = jnp.broadcast_to(sums[b : b + 1], (128, 128)).T
        square = jnp.broadcast_to(sums[blocks + b : blocks + b + 1], (128, 128)).T
        scale = lax.rsqrt(square - mean * mean + 1e-05)
        at = pl.ds(b * 128, 128)
        for k in range(hidden.shape[1] // 128):
            lanes = pl.ds(k * 128, 128)
            out[at, lanes] = (hidden[at, lanes] - mean) * scale * gain[:, lanes]


def normalise(hidden, own, other, gain, width):
    def kernel(*refs):
        norm_kernel(width, *refs)

    return pl.pallas_call(
        kernel,
        out_shape=jax.ShapeDtypeStruct(hidden.shape, F32),
        in_specs=[VMEM] * 4,
        out_specs=VMEM,
        name="normalise",
        compiler_params=pltpu.CompilerParams(vmem_limit_bytes=16 << 20),
    )(hidden, own, other, gain[None, :])


def neighbours(first, last):
    doms = NX * NYL * NZ * NC
    prev = lax.ppermute(last, "dom", [(i, i + 1) for i in range(doms - 1)])
    after = lax.ppermute(first, "dom", [(i + 1, i) for i in range(doms - 1)])
    return prev, after


def shards(
    features,
    infill_mask,
    mask_token,
    local_rows,
    local_cols,
    local_tiles,
    hub_ids,
    hub_count,
    hub_rows,
    hub_panels,
    hub_tiles,
    mix_weight,
    mix_bias,
    norm_gain,
):
    rows, half = features.shape
    blocks = rows // 128
    edge = 512

    own_f = hub_rows_of(hub_ids, infill_mask, features, mask_token)
    own_g = send(own_f, lambda x, yl, z, c, f: (x, yl, z, c, 1 - f))
    other_f = send(own_f, lambda x, yl, z, c, f: (x, 1 - yl, z, c, f))
    other_g = send(own_f, lambda x, yl, z, c, f: (x, 1 - yl, z, c, 1 - f))

    filled = jnp.where(infill_mask[:, None] == 1, mask_token[None, :], features)
    filled, own_f = lax.optimization_barrier((filled, own_f))
    first, mid, last = filled[:edge], filled[edge : rows - edge], filled[rows - edge :]
    swap = lambda v: send(v, lambda x, yl, z, c, f: (x, yl, z, c, 1 - f))
    first_g, last_g, mid_g = swap(first), swap(last), swap(mid)

    y_hub = mix_hub(own_f, own_g, other_f, other_g, mix_weight)
    stack = [y_hub]
    for d in range(1, NZ):
        stack.append(send(y_hub, lambda x, yl, z, c, f: (x, yl, z + d, c, f)))
    line = jnp.stack(stack, 0)
    parts = [line]
    for d in range(1, NX):
        parts.append(send(line, lambda x, yl, z, c, f: (x + d, yl, z, c, f)))
    parts = parts + [send(v, lambda x, yl, z, c, f: (x, yl, z, 1 - c, f)) for v in parts]

    y_first = mix(first, first_g, mix_weight)
    y_last = mix(last, last_g, mix_weight)
    prev, after = neighbours(y_first, y_last)
    y_mid = mix(mid, mid_g, mix_weight)
    total = local_sum(
        local_rows, local_cols, local_tiles[0], (prev, y_first, y_mid, y_last, after), blocks
    )
    hidden, stats = hub_and_hidden(
        hub_count, hub_rows, hub_panels, hub_tiles[0], total, filled, mix_bias, parts
    )
    stats_g = swap(stats)
    return normalise(hidden, stats, stats_g, norm_gain, half * lax.axis_size("feat"))


def solution(mesh):
    in_specs = (
        P("dom", "feat"),
        P("dom"),
        P("feat"),
        P("dom", None),
        P("dom", None),
        P("dom", None, None, None),
        P("dom"),
        P("dom"),
        P("dom", None),
        P("dom", None),
        P("dom", None, None, None),
        P(None, "feat"),
        P("feat"),
        P("feat"),
    )
    out_specs = P("dom", "feat")
    return jax.shard_map(shards, mesh=mesh, in_specs=in_specs, out_specs=out_specs, check_vma=False)
```

```python
import functools

import jax
import jax.numpy as jnp
from jax import lax
from jax.experimental import pallas as pl
from jax.experimental.pallas import tpu as pltpu
from jax.sharding import PartitionSpec as P

NX, NYL, NZ, NC = 4, 2, 8, 2
BOTH = ("dom", "feat")
F32 = jnp.float32
BF = jnp.bfloat16
SMEM = pl.BlockSpec(memory_space=pltpu.SMEM)
VMEM = pl.BlockSpec(memory_space=pltpu.VMEM)
ANY = pl.BlockSpec(memory_space=pl.ANY)
LIGHT = pl.CostEstimate(flops=1, bytes_accessed=1, transcendentals=0)


def dom_index(x, yl, z, c):
    return ((x * NYL + yl) * NZ + z) * NC + c


def shift(move):
    pairs = []
    for x in range(NX):
        for yl in range(NYL):
            for z in range(NZ):
                for c in range(NC):
                    for f in range(2):
                        tx, tyl, tz, tc, tf = move(x, yl, z, c, f)
                        pairs.append(
                            (
                                dom_index(x, yl, z, c) * 2 + f,
                                dom_index(tx % NX, tyl, tz % NZ, tc) * 2 + tf,
                            )
                        )
    return pairs


def send(value, move):
    return lax.ppermute(value, BOTH, shift(move))


def place():
    dom = lax.axis_index("dom")
    c = dom % NC
    z = (dom // NC) % NZ
    yl = (dom // (NC * NZ)) % NYL
    x = dom // (NC * NZ * NYL)
    return x, yl, z, c


def split(a):
    hi = a.astype(BF)
    return hi, (a - hi.astype(F32)).astype(BF)


def dot(a, b):
    return jnp.dot(a, b, preferred_element_type=F32)


def hub_rows_kernel(ids, mask, features, token, out, sems):
    first = lax.axis_index("dom") * features.shape[0]
    count = ids.shape[0]
    copies = []
    for i in range(count):
        row = ids[i] - first
        copies.append(
            pltpu.make_async_copy(features.at[pl.ds(row, 1)], out.at[pl.ds(i, 1)], sems.at[i])
        )
        copies[-1].start()
    out[pl.ds(count, 8), :] = jnp.broadcast_to(token[...], (8, token.shape[1]))
    for i in range(count):
        copies[i].wait()
    for i in range(count):
        row = ids[i] - first
        here = pl.ds(i, 1)
        out[here, :] = jnp.where(mask[row] == 1, token[...], out[here, :])


def hub_rows_of(hub_ids, infill_mask, features, mask_token):
    count = hub_ids.shape[0]
    half = features.shape[1]
    return pl.pallas_call(
        hub_rows_kernel,
        out_shape=jax.ShapeDtypeStruct((count + 8, half), F32),
        in_specs=[SMEM, SMEM, ANY, VMEM],
        out_specs=VMEM,
        scratch_shapes=[pltpu.SemaphoreType.DMA((count,))],
        name="hub_rows",
        cost_estimate=LIGHT,
    )(hub_ids, infill_mask, features, mask_token[None, :])


def mix_rows(xf, xg, weight):
    f = lax.axis_index("feat")
    half = xf.shape[1]
    wf = weight[pl.ds(pl.multiple_of(f * half, half), half), :]
    wg = weight[pl.ds(pl.multiple_of((1 - f) * half, half), half), :]
    wfh, wfl = split(wf)
    wgh, wgl = split(wg)
    right = jnp.concatenate([wfh, wfl, wfh, wgh, wgl, wgh], 0)
    fh, fl = split(xf)
    gh, gl = split(xg)
    left = jnp.concatenate([fh, fh, fl, gh, gh, gl], 1)
    return dot(left, right)


def chosen(y, mask_row, token_y):
    here = jnp.broadcast_to(mask_row, (128, 128)).T
    halves = []
    for k in range(y.shape[1] // 128):
        lanes = slice(k * 128, (k + 1) * 128)
        halves.append(jnp.where(here == 1.0, token_y[:, lanes], y[:, lanes]))
    return jnp.concatenate(halves, 1)


def mix_into(xf, xg, weight, mask, token_y, store):
    step = 256
    for i in range(xf.shape[0] // step):
        at = pl.ds(i * step, step)
        y = mix_rows(xf[at, :], xg[at, :], weight)
        for j in range(step // 128):
            b = i * (step // 128) + j
            store(b, chosen(y[j * 128 : (j + 1) * 128], mask[b : b + 1, :], token_y[:1, :]))


def mix_kernel(xf, xg, weight, mask, token_y, *outs):
    def store(b, y):
        for out in outs:
            n = out.shape[0] // 128
            if 0 <= b < n:
                out[pl.ds(b * 128, 128), :] = y
            b -= n

    mix_into(xf, xg, weight, mask[...].astype(F32), token_y, store)


def mix(xf, xg, weight, mask, token_y, sizes):
    rows, half = xf.shape
    return pl.pallas_call(
        mix_kernel,
        out_shape=[jax.ShapeDtypeStruct((size, half), F32) for size in sizes],
        in_specs=[VMEM] * 5,
        out_specs=[VMEM] * len(sizes),
        name="mix_rows",
        cost_estimate=LIGHT,
        compiler_params=pltpu.CompilerParams(vmem_limit_bytes=16 << 20),
    )(xf, xg, weight, mask, token_y)


def mix_hub_kernel(own_f, own_g, other_f, other_g, weight, out, token_y):
    count = own_f.shape[0] - 8
    yl = place()[1]
    xf = jnp.concatenate([own_f[...], other_f[:count]], 0)
    xg = jnp.concatenate([own_g[...], other_g[:count]], 0)
    y = mix_rows(xf, xg, weight)
    out[pl.ds(pl.multiple_of(yl * count, count), count), :] = y[:count]
    token_y[...] = y[count : count + 8]
    out[pl.ds(pl.multiple_of((1 - yl) * count, count), count), :] = y[count + 8 :]


def mix_hub(own_f, own_g, other_f, other_g, weight):
    count, half = own_f.shape[0] - 8, own_f.shape[1]
    return pl.pallas_call(
        mix_hub_kernel,
        out_shape=[
            jax.ShapeDtypeStruct((2 * count, half), F32),
            jax.ShapeDtypeStruct((8, half), F32),
        ],
        in_specs=[VMEM] * 5,
        out_specs=[VMEM, VMEM],
        name="mix_hub",
        cost_estimate=LIGHT,
    )(own_f, own_g, other_f, other_g, weight)


def tile_product(tile, y):
    ah, al = split(tile)
    yh, yl = split(y)
    return dot(jnp.concatenate([ah, ah, al], 1), jnp.concatenate([yh, yl, yh], 0))


UNROLL = 8


def gathered_sum(count, index, row_of, tile_of, y_of, total):
    def step(i, carry):
        products, rows = [], []
        for u in range(UNROLL):
            k = i * UNROLL + u
            t = index(k)
            product = tile_product(tile_of(t), y_of(t))
            products.append(jnp.where(k < count, product, 0.0))
            rows.append(row_of(t))
        for u in range(UNROLL):
            total[rows[u]] += products[u]
        return carry

    lax.fori_loop(0, (count + UNROLL - 1) // UNROLL, step, 0)


def list_tiles(cols, wanted, listed):
    def clear(t, carry):
        listed[t] = 0
        return carry

    def step(t, n):
        listed[n] = t
        return n + jnp.where(wanted(cols[0, t]), 1, 0)

    lax.fori_loop(0, listed.shape[0], clear, 0)
    return lax.fori_loop(0, cols.shape[1], step, 0)


def inside(col, low, high):
    return jnp.logical_and(col >= low, col < high)


def fill_blocks(ext, at, parts):
    for part in parts:
        n = part.shape[0] // 128
        ext[pl.ds(at, n)] = part[...].reshape(n, 128, part.shape[1])
        at += n


def early_kernel(late, rows, cols, tiles, *rest):
    parts, (total, ext, listed) = rest[:-3], rest[-3:]
    total[...] = jnp.zeros_like(total)
    low, high = late
    blocks = total.shape[0]
    fill_blocks(ext, 0, parts)

    def wanted(col):
        return jnp.logical_or(inside(col, blocks, low), inside(col, high, 2 * blocks))

    def y_of(t):
        col = cols[0, t]
        at = col - blocks - jnp.where(col >= high, high - low, 0)
        return ext[jnp.clip(at, 0, ext.shape[0] - 1)]

    count = list_tiles(cols, wanted, listed)
    gathered_sum(
        count, lambda k: listed[k], lambda t: rows[0, t], lambda t: tiles[t], y_of, total
    )


def early_sum(late, rows, cols, tiles, parts, blocks):
    half = parts[0].shape[1]
    depth = sum(p.shape[0] for p in parts) // 128
    count = tiles.shape[0]
    return pl.pallas_call(
        functools.partial(early_kernel, late),
        out_shape=jax.ShapeDtypeStruct((blocks, 128, half), F32),
        in_specs=[SMEM, SMEM] + [VMEM] * (1 + len(parts)),
        out_specs=VMEM,
        scratch_shapes=[
            pltpu.VMEM((depth, 128, half), F32),
            pltpu.SMEM((count + UNROLL,), jnp.int32),
        ],
        name="early_tiles",
        cost_estimate=LIGHT,
        compiler_params=pltpu.CompilerParams(vmem_limit_bytes=24 << 20),
    )(rows, cols, tiles, *parts)


def late_kernel(
    late, rows, cols, tiles, prev, after, xf, xg, weight, mask, token_y, total_in, total, ext, listed
):
    total[...] = total_in[...]
    low, high = late
    marks = mask[...].astype(F32)
    blocks = total.shape[0]
    size = high - low
    reach = prev.shape[0] // 128
    fill_blocks(ext, size, (prev, after))

    def store(b, y):
        ext[b] = y

    mix_into(xf, xg, weight, marks[low - blocks : high - blocks], token_y, store)

    def wanted(col):
        return jnp.logical_or(
            inside(col, low, high), jnp.logical_or(col < blocks, col >= 2 * blocks)
        )

    def y_of(t):
        col = cols[0, t]
        at = jnp.where(
            col < blocks,
            size + col - (blocks - reach),
            jnp.where(col >= 2 * blocks, size + reach + col - 2 * blocks, col - low),
        )
        return ext[jnp.clip(at, 0, ext.shape[0] - 1)]

    count = list_tiles(cols, wanted, listed)
    gathered_sum(
        count, lambda k: listed[k], lambda t: rows[0, t], lambda t: tiles[t], y_of, total
    )


def late_sum(late, rows, cols, tiles, prev, after, xf, xg, weight, mask, token_y, total):
    half = xf.shape[1]
    count = tiles.shape[0]
    depth = late[1] - late[0] + (prev.shape[0] + after.shape[0]) // 128
    return pl.pallas_call(
        functools.partial(late_kernel, late),
        out_shape=jax.ShapeDtypeStruct(total.shape, F32),
        in_specs=[SMEM, SMEM] + [VMEM] * 9,
        out_specs=VMEM,
        scratch_shapes=[
            pltpu.VMEM((depth, 128, half), F32),
            pltpu.SMEM((count + UNROLL,), jnp.int32),
        ],
        name="late_tiles",
        cost_estimate=LIGHT,
        compiler_params=pltpu.CompilerParams(vmem_limit_bytes=24 << 20),
    )(rows, cols, tiles, prev, after, xf, xg, weight, mask, token_y, total)


PART_AT = (0, 2, 3, 4, 6)


def final_kernel(
    live_ref, hub_rows, panels, hub_tiles, mask, token, total_in, features, bias, *rest
):
    parts = rest[:-5]
    hidden, stats, total, held, sems = rest[-5:]
    copies = []
    for k, (part, at) in enumerate(zip(parts, PART_AT)):
        to = held.at[pl.ds(at, 2)] if len(part.shape) == 3 else held.at[at]
        copies.append(pltpu.make_async_copy(part, to, sems.at[k]))
        copies[-1].start()
    total[...] = total_in[...]
    marks = mask[...].astype(F32)
    blocks = total.shape[0]
    for copy in copies:
        copy.wait()
    x, yl, z, c = place()
    hubs = 32

    def panel(t):
        p = panels[0, t]
        px = p // 8
        pyl = (p // 4) % 2
        kx = (px - x + NX) % NX
        slabs = []
        for k in range(4):
            pz = 2 * (p % 4) + k // 2
            pc = k % 2
            kind = (pz - z + NZ) % 4
            offset = jnp.where(kind < 2, kind, kind - 4)
            far = ((pz - z - offset + 2 * NZ) % NZ) // 4
            unit = jnp.where(kind == 0, 0, jnp.where(kind == 3, 1, kind + 1))
            unit = jnp.where(kind == 2, 3, unit)
            holder = jnp.where(kx == 3, 0, 1)
            other = 4 + jnp.where(holder == c, 0, 2) + jnp.where(holder == pc, 0, 1)
            slot = jnp.where(kx % 2 == 1, other, kx + (pc + c) % 2)
            row = unit * 128 + far * 64 + pyl * hubs
            slabs.append(held[slot, pl.ds(pl.multiple_of(row, hubs), hubs), :])
        return jnp.concatenate(slabs, 0)

    gathered_sum(
        live_ref[0],
        lambda k: k,
        lambda t: hub_rows[0, t],
        lambda t: hub_tiles[t],
        panel,
        total,
    )
    for b in range(blocks):
        at = pl.ds(b * 128, 128)
        v = total[b] + bias[...]
        filled = chosen(features[at, :], marks[b : b + 1, :], token[...])
        h = filled + v / (1.0 + jnp.exp(-v))
        hidden[at, :] = h
        q = h * h
        s = h[:, :128] + h[:, 128:]
        q = q[:, :128] + q[:, 128:]
        stats[pl.ds(b, 1), :] = jnp.sum(s.T, 0, keepdims=True)
        stats[pl.ds(blocks + b, 1), :] = jnp.sum(q.T, 0, keepdims=True)


def final(scalars, arrays, parts):
    total, features = arrays[3], arrays[4]
    blocks, _, half = total.shape
    n = features.shape[0]
    return pl.pallas_call(
        final_kernel,
        out_shape=[
            jax.ShapeDtypeStruct((n, half), F32),
            jax.ShapeDtypeStruct((2 * blocks, 128), F32),
        ],
        in_specs=[SMEM] * len(scalars) + [VMEM] * len(arrays) + [ANY] * len(parts),
        out_specs=[VMEM, VMEM],
        scratch_shapes=[
            pltpu.VMEM((blocks, 128, half), F32),
            pltpu.VMEM((2 * NX,) + parts[1].shape, F32),
            pltpu.SemaphoreType.DMA((len(parts),)),
        ],
        name="final_tiles",
        cost_estimate=LIGHT,
        compiler_params=pltpu.CompilerParams(vmem_limit_bytes=32 << 20),
    )(*scalars, *arrays, *parts)


def norm_kernel(width, hidden, own, other, gain, out):
    blocks = own.shape[0] // 2
    sums = (own[...] + other[...]) / width
    for b in range(blocks):
        mean = jnp.broadcast_to(sums[b : b + 1], (128, 128)).T
        square = jnp.broadcast_to(sums[blocks + b : blocks + b + 1], (128, 128)).T
        scale = lax.rsqrt(square - mean * mean + 1e-05)
        at = pl.ds(b * 128, 128)
        for k in range(hidden.shape[1] // 128):
            lanes = pl.ds(k * 128, 128)
            out[at, lanes] = (hidden[at, lanes] - mean) * scale * gain[:, lanes]


def normalise(hidden, own, other, gain, width):
    def kernel(*refs):
        norm_kernel(width, *refs)

    return pl.pallas_call(
        kernel,
        out_shape=jax.ShapeDtypeStruct(hidden.shape, F32),
        in_specs=[VMEM] * 4,
        out_specs=VMEM,
        name="normalise",
        cost_estimate=LIGHT,
        compiler_params=pltpu.CompilerParams(vmem_limit_bytes=16 << 20),
    )(hidden, own, other, gain[None, :])


def neighbours(first, last):
    doms = NX * NYL * NZ * NC
    prev = lax.ppermute(last, "dom", [(i, i + 1) for i in range(doms - 1)])
    after = lax.ppermute(first, "dom", [(i + 1, i) for i in range(doms - 1)])
    return prev, after


def shards(
    features,
    infill_mask,
    mask_token,
    local_rows,
    local_cols,
    local_tiles,
    hub_ids,
    hub_count,
    hub_rows,
    hub_panels,
    hub_tiles,
    mix_weight,
    mix_bias,
    norm_gain,
):
    rows, half = features.shape
    blocks = rows // 128
    edge = 512
    wide = 640
    inner = wide - edge
    bounds = (((0, wide), (rows - wide, wide)), ((wide, rows - 2 * wide),))
    mask = infill_mask.reshape(blocks, 128)
    swap = lambda v: send(v, lambda x, yl, z, c, f: (x, yl, z, c, 1 - f))

    own_f = hub_rows_of(hub_ids, infill_mask, features, mask_token)
    own_g = swap(own_f)
    other_f = send(own_f, lambda x, yl, z, c, f: (x, 1 - yl, z, c, f))
    other_g = send(own_f, lambda x, yl, z, c, f: (x, 1 - yl, z, c, 1 - f))
    chunks = [
        jnp.concatenate([features[low : low + size] for low, size in ranges], 0)
        for ranges in bounds
    ]
    chunks, own_g, other_f, other_g = lax.optimization_barrier((chunks, own_g, other_f, other_g))
    chunks_g = [swap(v) for v in chunks]

    y_hub, token_y = mix_hub(own_f, own_g, other_f, other_g, mix_weight)
    own = jnp.concatenate([y_hub, send(y_hub, lambda x, yl, z, c, f: (x, yl, z + 4, c, f))], 0)
    units = [own] + [
        send(own, lambda x, yl, z, c, f: (x, yl, z + d, c, f)) for d in (1, -1, 2)
    ]
    line = jnp.concatenate(units, 0)
    sibling = lambda v: send(v, lambda x, yl, z, c, f: (x, yl, z, 1 - c, f))
    across = send(line, lambda x, yl, z, c, f: (x + 2, yl, z, c, f))
    line_s, chunks_g[0], = lax.optimization_barrier((sibling(line), chunks_g[0]))
    pair = jnp.stack([line, line_s], 0)
    beside = send(pair, lambda x, yl, z, c, f: (x + 1 - 2 * c, yl, z, c, f))

    marks = jnp.concatenate(
        [mask[low // 128 : (low + size) // 128] for low, size in bounds[0]], 0
    )
    y_first, y_left, y_right, y_last = mix(
        chunks[0], chunks_g[0], mix_weight, marks, token_y, (edge, inner, inner, edge)
    )
    prev, after = neighbours(y_first, y_last)
    late = (blocks + wide // 128, 2 * blocks - wide // 128)
    total = early_sum(
        late,
        local_rows,
        local_cols,
        local_tiles[0],
        (y_first, y_left, y_right, y_last),
        blocks,
    )
    across, beside, total, chunks_g[1], prev, after = lax.optimization_barrier(
        (across, beside, total, chunks_g[1], prev, after)
    )
    parts = (pair, across, sibling(across), beside, sibling(beside))
    total = late_sum(
        late,
        local_rows,
        local_cols,
        local_tiles[0],
        prev,
        after,
        chunks[1],
        chunks_g[1],
        mix_weight,
        mask,
        token_y,
        total,
    )
    hidden, stats = final(
        (hub_count, hub_rows, hub_panels),
        (hub_tiles[0], mask, mask_token[None, :], total, features, mix_bias[None, :]),
        parts,
    )
    return normalise(hidden, stats, swap(stats), norm_gain, half * lax.axis_size("feat"))


def solution(mesh):
    in_specs = (
        P("dom", "feat"),
        P("dom"),
        P("feat"),
        P("dom", None),
        P("dom", None),
        P("dom", None, None, None),
        P("dom"),
        P("dom"),
        P("dom", None),
        P("dom", None),
        P("dom", None, None, None),
        P(None, "feat"),
        P("feat"),
        P("feat"),
    )
    out_specs = P("dom", "feat")
    return jax.shard_map(shards, mesh=mesh, in_specs=in_specs, out_specs=out_specs, check_vma=False)
```

```python
import functools

import jax
import jax.numpy as jnp
from jax import lax
from jax.experimental import pallas as pl
from jax.experimental.pallas import tpu as pltpu
from jax.sharding import PartitionSpec as P

NX, NYL, NZ, NC = 4, 2, 8, 2
BOTH = ("dom", "feat")
F32 = jnp.float32
BF = jnp.bfloat16
SMEM = pl.BlockSpec(memory_space=pltpu.SMEM)
VMEM = pl.BlockSpec(memory_space=pltpu.VMEM)
ANY = pl.BlockSpec(memory_space=pl.ANY)
LIGHT = pl.CostEstimate(flops=1, bytes_accessed=1, transcendentals=0)


def dom_index(x, yl, z, c):
    return ((x * NYL + yl) * NZ + z) * NC + c


def shift(move):
    pairs = []
    for x in range(NX):
        for yl in range(NYL):
            for z in range(NZ):
                for c in range(NC):
                    for f in range(2):
                        tx, tyl, tz, tc, tf = move(x, yl, z, c, f)
                        pairs.append(
                            (
                                dom_index(x, yl, z, c) * 2 + f,
                                dom_index(tx % NX, tyl, tz % NZ, tc) * 2 + tf,
                            )
                        )
    return pairs


def send(value, move):
    return lax.ppermute(value, BOTH, shift(move))


def place():
    dom = lax.axis_index("dom")
    c = dom % NC
    z = (dom // NC) % NZ
    yl = (dom // (NC * NZ)) % NYL
    x = dom // (NC * NZ * NYL)
    return x, yl, z, c


def split(a):
    hi = a.astype(BF)
    return hi, (a - hi.astype(F32)).astype(BF)


def dot(a, b):
    return jnp.dot(a, b, preferred_element_type=F32)


def hub_rows_kernel(ids, mask, features, token, out, sems):
    first = lax.axis_index("dom") * features.shape[0]
    count = ids.shape[0]
    copies = []
    for i in range(count):
        row = ids[i] - first
        copies.append(
            pltpu.make_async_copy(features.at[pl.ds(row, 1)], out.at[pl.ds(i, 1)], sems.at[i])
        )
        copies[-1].start()
    out[pl.ds(count, 8), :] = jnp.broadcast_to(token[...], (8, token.shape[1]))
    for i in range(count):
        copies[i].wait()
    for i in range(count):
        row = ids[i] - first
        here = pl.ds(i, 1)
        out[here, :] = jnp.where(mask[row] == 1, token[...], out[here, :])


def hub_rows_of(hub_ids, infill_mask, features, mask_token):
    count = hub_ids.shape[0]
    half = features.shape[1]
    return pl.pallas_call(
        hub_rows_kernel,
        out_shape=jax.ShapeDtypeStruct((count + 8, half), F32),
        in_specs=[SMEM, SMEM, ANY, VMEM],
        out_specs=VMEM,
        scratch_shapes=[pltpu.SemaphoreType.DMA((count,))],
        name="hub_rows",
        cost_estimate=LIGHT,
    )(hub_ids, infill_mask, features, mask_token[None, :])


def mix_rows(xf, xg, weight):
    f = lax.axis_index("feat")
    half = xf.shape[1]
    wf = weight[pl.ds(pl.multiple_of(f * half, half), half), :]
    wg = weight[pl.ds(pl.multiple_of((1 - f) * half, half), half), :]
    wfh, wfl = split(wf)
    wgh, wgl = split(wg)
    right = jnp.concatenate([wfh, wfl, wfh, wgh, wgl, wgh], 0)
    fh, fl = split(xf)
    gh, gl = split(xg)
    left = jnp.concatenate([fh, fh, fl, gh, gh, gl], 1)
    return dot(left, right)


def chosen(y, mask_row, token_y):
    here = jnp.broadcast_to(mask_row, (128, 128)).T
    halves = []
    for k in range(y.shape[1] // 128):
        lanes = slice(k * 128, (k + 1) * 128)
        halves.append(jnp.where(here == 1.0, token_y[:, lanes], y[:, lanes]))
    return jnp.concatenate(halves, 1)


def mix_into(xf, xg, weight, mask, token_y, store):
    step = 256
    for i in range(xf.shape[0] // step):
        at = pl.ds(i * step, step)
        y = mix_rows(xf[at, :], xg[at, :], weight)
        for j in range(step // 128):
            b = i * (step // 128) + j
            store(b, chosen(y[j * 128 : (j + 1) * 128], mask[b : b + 1, :], token_y[:1, :]))


def mix_kernel(xf, xg, weight, mask, token_y, *outs):
    def store(b, y):
        for out in outs:
            n = out.shape[0] // 128
            if 0 <= b < n:
                out[pl.ds(b * 128, 128), :] = y
            b -= n

    mix_into(xf, xg, weight, mask[...].astype(F32), token_y, store)


def mix(xf, xg, weight, mask, token_y, sizes):
    rows, half = xf.shape
    return pl.pallas_call(
        mix_kernel,
        out_shape=[jax.ShapeDtypeStruct((size, half), F32) for size in sizes],
        in_specs=[VMEM] * 5,
        out_specs=[VMEM] * len(sizes),
        name="mix_rows",
        cost_estimate=LIGHT,
        compiler_params=pltpu.CompilerParams(vmem_limit_bytes=16 << 20),
    )(xf, xg, weight, mask, token_y)


def mix_hub_kernel(own_f, own_g, other_f, other_g, weight, out, token_y):
    count = own_f.shape[0] - 8
    yl = place()[1]
    xf = jnp.concatenate([own_f[...], other_f[:count]], 0)
    xg = jnp.concatenate([own_g[...], other_g[:count]], 0)
    y = mix_rows(xf, xg, weight)
    out[pl.ds(pl.multiple_of(yl * count, count), count), :] = y[:count]
    token_y[...] = y[count : count + 8]
    out[pl.ds(pl.multiple_of((1 - yl) * count, count), count), :] = y[count + 8 :]


def mix_hub(own_f, own_g, other_f, other_g, weight):
    count, half = own_f.shape[0] - 8, own_f.shape[1]
    return pl.pallas_call(
        mix_hub_kernel,
        out_shape=[
            jax.ShapeDtypeStruct((2 * count, half), F32),
            jax.ShapeDtypeStruct((8, half), F32),
        ],
        in_specs=[VMEM] * 5,
        out_specs=[VMEM, VMEM],
        name="mix_hub",
        cost_estimate=LIGHT,
    )(own_f, own_g, other_f, other_g, weight)


def tile_product(tile, y):
    ah, al = split(tile)
    yh, yl = split(y)
    return dot(jnp.concatenate([ah, ah, al], 1), jnp.concatenate([yh, yl, yh], 0))


UNROLL = 8


def gathered_sum(count, index, row_of, tile_of, y_of, total):
    def step(i, carry):
        products, rows = [], []
        for u in range(UNROLL):
            k = i * UNROLL + u
            t = index(k)
            product = tile_product(tile_of(t), y_of(t))
            products.append(jnp.where(k < count, product, 0.0))
            rows.append(row_of(t))
        for u in range(UNROLL):
            total[rows[u]] += products[u]
        return carry

    lax.fori_loop(0, (count + UNROLL - 1) // UNROLL, step, 0)


def list_tiles(wanted, listed):
    def clear(t, carry):
        listed[t] = 0
        return carry

    def step(t, n):
        listed[n] = t
        return n + jnp.where(wanted(t), 1, 0)

    lax.fori_loop(0, listed.shape[0], clear, 0)
    return lax.fori_loop(0, listed.shape[0] - UNROLL, step, 0)


def inside(col, low, high):
    return jnp.logical_and(col >= low, col < high)


def fill_blocks(ext, at, parts):
    for part in parts:
        n = part.shape[0] // 128
        ext[pl.ds(at, n)] = part[...].reshape(n, 128, part.shape[1])
        at += n


def early_kernel(late, rows, cols, tiles, *rest):
    parts, (total, ext, listed) = rest[:-3], rest[-3:]
    total[...] = jnp.zeros_like(total)
    low, high = late
    blocks = total.shape[0]
    fill_blocks(ext, 0, parts)

    def wanted(t):
        col = cols[0, t]
        return jnp.logical_or(inside(col, blocks, low), inside(col, high, 2 * blocks))

    def y_of(t):
        col = cols[0, t]
        at = col - blocks - jnp.where(col >= high, high - low, 0)
        return ext[jnp.clip(at, 0, ext.shape[0] - 1)]

    count = list_tiles(wanted, listed)
    gathered_sum(
        count, lambda k: listed[k], lambda t: rows[0, t], lambda t: tiles[t], y_of, total
    )


def early_sum(late, rows, cols, tiles, parts, blocks):
    half = parts[0].shape[1]
    depth = sum(p.shape[0] for p in parts) // 128
    count = tiles.shape[0]
    return pl.pallas_call(
        functools.partial(early_kernel, late),
        out_shape=jax.ShapeDtypeStruct((blocks, 128, half), F32),
        in_specs=[SMEM, SMEM] + [VMEM] * (1 + len(parts)),
        out_specs=VMEM,
        scratch_shapes=[
            pltpu.VMEM((depth, 128, half), F32),
            pltpu.SMEM((count + UNROLL,), jnp.int32),
        ],
        name="early_tiles",
        cost_estimate=LIGHT,
        compiler_params=pltpu.CompilerParams(vmem_limit_bytes=24 << 20),
    )(rows, cols, tiles, *parts)


def late_kernel(
    late, rows, cols, tiles, prev, after, y_mid, total_in, total, ext, listed
):
    total[...] = total_in[...]
    low, high = late
    blocks = total.shape[0]
    size = high - low
    reach = prev.shape[0] // 128
    fill_blocks(ext, 0, (y_mid, prev, after))

    def wanted(t):
        col = cols[0, t]
        return jnp.logical_or(
            inside(col, low, high), jnp.logical_or(col < blocks, col >= 2 * blocks)
        )

    def y_of(t):
        col = cols[0, t]
        at = jnp.where(
            col < blocks,
            size + col - (blocks - reach),
            jnp.where(col >= 2 * blocks, size + reach + col - 2 * blocks, col - low),
        )
        return ext[jnp.clip(at, 0, ext.shape[0] - 1)]

    count = list_tiles(wanted, listed)
    gathered_sum(
        count, lambda k: listed[k], lambda t: rows[0, t], lambda t: tiles[t], y_of, total
    )


def late_sum(late, rows, cols, tiles, prev, after, y_mid, total):
    half = y_mid.shape[1]
    count = tiles.shape[0]
    depth = late[1] - late[0] + (prev.shape[0] + after.shape[0]) // 128
    return pl.pallas_call(
        functools.partial(late_kernel, late),
        out_shape=jax.ShapeDtypeStruct(total.shape, F32),
        in_specs=[SMEM, SMEM] + [VMEM] * 5,
        out_specs=VMEM,
        scratch_shapes=[
            pltpu.VMEM((depth, 128, half), F32),
            pltpu.SMEM((count + UNROLL,), jnp.int32),
        ],
        name="late_tiles",
        cost_estimate=LIGHT,
        compiler_params=pltpu.CompilerParams(vmem_limit_bytes=24 << 20),
    )(rows, cols, tiles, prev, after, y_mid, total)


UNIT_OF_KIND = 0b01111000
PART_AT = (0, 2, 3, 4, 6)


def final_kernel(
    live_ref, hub_rows, panels, hub_tiles, mask, token, total_in, features, bias, *rest
):
    parts = rest[:-5]
    hidden, stats, total, held, sems = rest[-5:]
    copies = []
    for k, (part, at) in enumerate(zip(parts, PART_AT)):
        to = held.at[pl.ds(at, 2)] if len(part.shape) == 3 else held.at[at]
        copies.append(pltpu.make_async_copy(part, to, sems.at[k]))
        copies[-1].start()
    total[...] = total_in[...]
    marks = mask[...].astype(F32)
    blocks = total.shape[0]
    for copy in copies:
        copy.wait()
    x, yl, z, c = place()
    hubs = 32

    def panel(t):
        p = panels[0, t]
        kx = ((p >> 3) - x) & 3
        holder = (kx >> 1) ^ 1
        odd = (kx & 1) == 1
        slots = [
            jnp.where(odd, 4 + 2 * (holder ^ c) + (holder ^ pc), kx + (pc ^ c)) for pc in range(2)
        ]
        slabs = []
        for dz in range(2):
            delta = 2 * (p & 3) + dz - z
            kind = delta & 3
            offset = ((kind + 2) & 3) - 2
            far = ((delta - offset) >> 2) & 1
            unit = (UNIT_OF_KIND >> (2 * kind)) & 3
            row = unit * 128 + far * 64 + ((p >> 2) & 1) * hubs
            for pc in range(2):
                slabs.append(held[slots[pc], pl.ds(pl.multiple_of(row, hubs), hubs), :])
        return jnp.concatenate(slabs, 0)

    gathered_sum(
        live_ref[0],
        lambda k: k,
        lambda t: hub_rows[0, t],
        lambda t: hub_tiles[t],
        panel,
        total,
    )
    for b in range(blocks):
        at = pl.ds(b * 128, 128)
        v = total[b] + bias[...]
        filled = chosen(features[at, :], marks[b : b + 1, :], token[...])
        h = filled + v / (1.0 + jnp.exp(-v))
        hidden[at, :] = h
        q = h * h
        s = h[:, :128] + h[:, 128:]
        q = q[:, :128] + q[:, 128:]
        stats[pl.ds(b, 1), :] = jnp.sum(s.T, 0, keepdims=True)
        stats[pl.ds(blocks + b, 1), :] = jnp.sum(q.T, 0, keepdims=True)


def final(scalars, arrays, parts):
    total, features = arrays[3], arrays[4]
    blocks, _, half = total.shape
    n = features.shape[0]
    return pl.pallas_call(
        final_kernel,
        out_shape=[
            jax.ShapeDtypeStruct((n, half), F32),
            jax.ShapeDtypeStruct((2 * blocks, 128), F32),
        ],
        in_specs=[SMEM] * len(scalars) + [VMEM] * len(arrays) + [ANY] * len(parts),
        out_specs=[VMEM, VMEM],
        scratch_shapes=[
            pltpu.VMEM((blocks, 128, half), F32),
            pltpu.VMEM((2 * NX,) + parts[1].shape, F32),
            pltpu.SemaphoreType.DMA((len(parts),)),
        ],
        name="final_tiles",
        cost_estimate=LIGHT,
        compiler_params=pltpu.CompilerParams(vmem_limit_bytes=32 << 20),
    )(*scalars, *arrays, *parts)


def norm_kernel(width, hidden, own, other, gain, out):
    blocks = own.shape[0] // 2
    sums = (own[...] + other[...]) / width
    for b in range(blocks):
        mean = jnp.broadcast_to(sums[b : b + 1], (128, 128)).T
        square = jnp.broadcast_to(sums[blocks + b : blocks + b + 1], (128, 128)).T
        scale = lax.rsqrt(square - mean * mean + 1e-05)
        at = pl.ds(b * 128, 128)
        for k in range(hidden.shape[1] // 128):
            lanes = pl.ds(k * 128, 128)
            out[at, lanes] = (hidden[at, lanes] - mean) * scale * gain[:, lanes]


def normalise(hidden, own, other, gain, width):
    def kernel(*refs):
        norm_kernel(width, *refs)

    return pl.pallas_call(
        kernel,
        out_shape=jax.ShapeDtypeStruct(hidden.shape, F32),
        in_specs=[VMEM] * 4,
        out_specs=VMEM,
        name="normalise",
        cost_estimate=LIGHT,
        compiler_params=pltpu.CompilerParams(vmem_limit_bytes=16 << 20),
    )(hidden, own, other, gain[None, :])


def neighbours(first, last):
    doms = NX * NYL * NZ * NC
    prev = lax.ppermute(last, "dom", [(i, i + 1) for i in range(doms - 1)])
    after = lax.ppermute(first, "dom", [(i + 1, i) for i in range(doms - 1)])
    return prev, after


def shards(
    features,
    infill_mask,
    mask_token,
    local_rows,
    local_cols,
    local_tiles,
    hub_ids,
    hub_count,
    hub_rows,
    hub_panels,
    hub_tiles,
    mix_weight,
    mix_bias,
    norm_gain,
):
    rows, half = features.shape
    blocks = rows // 128
    edge = 512
    wide = 640
    inner = wide - edge
    bounds = (((0, wide), (rows - wide, wide)), ((wide, rows - 2 * wide),))
    mask = infill_mask.reshape(blocks, 128)
    swap = lambda v: send(v, lambda x, yl, z, c, f: (x, yl, z, c, 1 - f))

    own_f = hub_rows_of(hub_ids, infill_mask, features, mask_token)
    own_g = swap(own_f)
    other_f = send(own_f, lambda x, yl, z, c, f: (x, 1 - yl, z, c, f))
    other_g = send(own_f, lambda x, yl, z, c, f: (x, 1 - yl, z, c, 1 - f))
    chunks = [
        jnp.concatenate([features[low : low + size] for low, size in ranges], 0)
        for ranges in bounds
    ]
    chunks, own_g, other_f, other_g = lax.optimization_barrier((chunks, own_g, other_f, other_g))
    chunks_g = [swap(v) for v in chunks]

    y_hub, token_y = mix_hub(own_f, own_g, other_f, other_g, mix_weight)
    own = jnp.concatenate([y_hub, send(y_hub, lambda x, yl, z, c, f: (x, yl, z + 4, c, f))], 0)
    units = [own] + [
        send(own, lambda x, yl, z, c, f: (x, yl, z + d, c, f)) for d in (1, -1, 2)
    ]
    line = jnp.concatenate(units, 0)
    sibling = lambda v: send(v, lambda x, yl, z, c, f: (x, yl, z, 1 - c, f))
    across = send(line, lambda x, yl, z, c, f: (x + 2, yl, z, c, f))
    line_s, chunks_g[0], = lax.optimization_barrier((sibling(line), chunks_g[0]))
    pair = jnp.stack([line, line_s], 0)
    beside = send(pair, lambda x, yl, z, c, f: (x + 1 - 2 * c, yl, z, c, f))

    marks = jnp.concatenate(
        [mask[low // 128 : (low + size) // 128] for low, size in bounds[0]], 0
    )
    y_first, y_left, y_right, y_last = mix(
        chunks[0], chunks_g[0], mix_weight, marks, token_y, (edge, inner, inner, edge)
    )
    late = (blocks + wide // 128, 2 * blocks - wide // 128)
    total = early_sum(
        late,
        local_rows,
        local_cols,
        local_tiles[0],
        (y_first, y_left, y_right, y_last),
        blocks,
    )
    across, y_first, y_last, total = lax.optimization_barrier((across, y_first, y_last, total))
    prev, after = neighbours(y_first, y_last)
    (y_mid,) = mix(
        chunks[1],
        chunks_g[1],
        mix_weight,
        mask[wide // 128 : blocks - wide // 128],
        token_y,
        (rows - 2 * wide,),
    )
    beside, y_mid, prev, after = lax.optimization_barrier((beside, y_mid, prev, after))
    parts = (pair, across, sibling(across), beside, sibling(beside))
    total = late_sum(
        late, local_rows, local_cols, local_tiles[0], prev, after, y_mid, total
    )
    hidden, stats = final(
        (hub_count, hub_rows, hub_panels),
        (hub_tiles[0], mask, mask_token[None, :], total, features, mix_bias[None, :]),
        parts,
    )
    return normalise(hidden, stats, swap(stats), norm_gain, half * lax.axis_size("feat"))


def solution(mesh):
    in_specs = (
        P("dom", "feat"),
        P("dom"),
        P("feat"),
        P("dom", None),
        P("dom", None),
        P("dom", None, None, None),
        P("dom"),
        P("dom"),
        P("dom", None),
        P("dom", None),
        P("dom", None, None, None),
        P(None, "feat"),
        P("feat"),
        P("feat"),
    )
    out_specs = P("dom", "feat")
    return jax.shard_map(shards, mesh=mesh, in_specs=in_specs, out_specs=out_specs, check_vma=False)
```

```python
import functools

import jax
import jax.numpy as jnp
from jax import lax
from jax.experimental import pallas as pl
from jax.experimental.pallas import tpu as pltpu
from jax.sharding import PartitionSpec as P

NX, NYL, NZ, NC = 4, 2, 8, 2
BOTH = ("dom", "feat")
F32 = jnp.float32
BF = jnp.bfloat16
SMEM = pl.BlockSpec(memory_space=pltpu.SMEM)
VMEM = pl.BlockSpec(memory_space=pltpu.VMEM)
ANY = pl.BlockSpec(memory_space=pl.ANY)
LIGHT = pl.CostEstimate(flops=1, bytes_accessed=1, transcendentals=0)


def dom_index(x, yl, z, c):
    return ((x * NYL + yl) * NZ + z) * NC + c


def shift(move):
    pairs = []
    for x in range(NX):
        for yl in range(NYL):
            for z in range(NZ):
                for c in range(NC):
                    for f in range(2):
                        tx, tyl, tz, tc, tf = move(x, yl, z, c, f)
                        pairs.append(
                            (
                                dom_index(x, yl, z, c) * 2 + f,
                                dom_index(tx % NX, tyl, tz % NZ, tc) * 2 + tf,
                            )
                        )
    return pairs


def send(value, move):
    return lax.ppermute(value, BOTH, shift(move))


def place():
    dom = lax.axis_index("dom")
    c = dom % NC
    z = (dom // NC) % NZ
    yl = (dom // (NC * NZ)) % NYL
    x = dom // (NC * NZ * NYL)
    return x, yl, z, c


def split(a):
    hi = a.astype(BF)
    return hi, (a - hi.astype(F32)).astype(BF)


def dot(a, b):
    return jnp.dot(a, b, preferred_element_type=F32)


def hub_rows_kernel(ids, mask, features, token, out, sems):
    first = lax.axis_index("dom") * features.shape[0]
    count = ids.shape[0]
    copies = []
    for i in range(count):
        row = ids[i] - first
        copies.append(
            pltpu.make_async_copy(features.at[pl.ds(row, 1)], out.at[pl.ds(i, 1)], sems.at[i])
        )
        copies[-1].start()
    out[pl.ds(count, 8), :] = jnp.broadcast_to(token[...], (8, token.shape[1]))
    for i in range(count):
        copies[i].wait()
    for i in range(count):
        row = ids[i] - first
        here = pl.ds(i, 1)
        out[here, :] = jnp.where(mask[row] == 1, token[...], out[here, :])


def hub_rows_of(hub_ids, infill_mask, features, mask_token):
    count = hub_ids.shape[0]
    half = features.shape[1]
    return pl.pallas_call(
        hub_rows_kernel,
        out_shape=jax.ShapeDtypeStruct((count + 8, half), F32),
        in_specs=[SMEM, SMEM, ANY, VMEM],
        out_specs=VMEM,
        scratch_shapes=[pltpu.SemaphoreType.DMA((count,))],
        name="hub_rows",
        cost_estimate=LIGHT,
    )(hub_ids, infill_mask, features, mask_token[None, :])


def mix_rows(xf, xg, weight):
    f = lax.axis_index("feat")
    half = xf.shape[1]
    wf = weight[pl.ds(pl.multiple_of(f * half, half), half), :]
    wg = weight[pl.ds(pl.multiple_of((1 - f) * half, half), half), :]
    wfh, wfl = split(wf)
    wgh, wgl = split(wg)
    right = jnp.concatenate([wfh, wfl, wfh, wgh, wgl, wgh], 0)
    fh, fl = split(xf)
    gh, gl = split(xg)
    left = jnp.concatenate([fh, fh, fl, gh, gh, gl], 1)
    return dot(left, right)


def columns(mask):
    n = mask.shape[0]
    pad = jnp.zeros((128 - n, 128), F32)
    return jnp.concatenate([mask[...].astype(F32), pad], 0).T


def chosen(y, column, token_y):
    return jnp.where(column == 1.0, token_y, y)


def mix_into(xf, xg, weight, mask, token_y, store):
    step = 256
    for i in range(xf.shape[0] // step):
        at = pl.ds(i * step, step)
        y = mix_rows(xf[at, :], xg[at, :], weight)
        for j in range(step // 128):
            b = i * (step // 128) + j
            store(b, chosen(y[j * 128 : (j + 1) * 128], mask[:, b : b + 1], token_y[:1, :]))


def mix_kernel(xf, xg, weight, mask, token_y, *outs):
    def store(b, y):
        for out in outs:
            n = out.shape[0] // 128
            if 0 <= b < n:
                out[pl.ds(b * 128, 128), :] = y
            b -= n

    mix_into(xf, xg, weight, columns(mask), token_y, store)


def mix(xf, xg, weight, mask, token_y, sizes):
    rows, half = xf.shape
    return pl.pallas_call(
        mix_kernel,
        out_shape=[jax.ShapeDtypeStruct((size, half), F32) for size in sizes],
        in_specs=[VMEM] * 5,
        out_specs=[VMEM] * len(sizes),
        name="mix_rows",
        cost_estimate=LIGHT,
        compiler_params=pltpu.CompilerParams(vmem_limit_bytes=16 << 20),
    )(xf, xg, weight, mask, token_y)


def mix_hub_kernel(own_f, own_g, other_f, other_g, weight, out, token_y):
    count = own_f.shape[0] - 8
    yl = place()[1]
    xf = jnp.concatenate([own_f[...], other_f[:count]], 0)
    xg = jnp.concatenate([own_g[...], other_g[:count]], 0)
    y = mix_rows(xf, xg, weight)
    out[pl.ds(pl.multiple_of(yl * count, count), count), :] = y[:count]
    token_y[...] = y[count : count + 8]
    out[pl.ds(pl.multiple_of((1 - yl) * count, count), count), :] = y[count + 8 :]


def mix_hub(own_f, own_g, other_f, other_g, weight):
    count, half = own_f.shape[0] - 8, own_f.shape[1]
    return pl.pallas_call(
        mix_hub_kernel,
        out_shape=[
            jax.ShapeDtypeStruct((2 * count, half), F32),
            jax.ShapeDtypeStruct((8, half), F32),
        ],
        in_specs=[VMEM] * 5,
        out_specs=[VMEM, VMEM],
        name="mix_hub",
        cost_estimate=LIGHT,
    )(own_f, own_g, other_f, other_g, weight)


def tile_product(tile, y):
    ah, al = split(tile)
    yh, yl = split(y)
    return dot(jnp.concatenate([ah, ah, al], 1), jnp.concatenate([yh, yl, yh], 0))


UNROLL = 8


def gathered_sum(count, index, row_of, tile_of, y_of, total):
    def step(i, carry):
        products, rows = [], []
        for u in range(UNROLL):
            k = i * UNROLL + u
            t = index(jnp.minimum(k, count - 1))
            product = tile_product(tile_of(t), y_of(t))
            products.append(jnp.where(k < count, product, 0.0))
            rows.append(row_of(t))
        for u in range(UNROLL):
            total[rows[u]] += products[u]
        return carry

    lax.fori_loop(0, (count + UNROLL - 1) // UNROLL, step, 0)


def list_tiles(wanted, listed):
    def step(t, n):
        listed[n] = t
        return n + jnp.where(wanted(t), 1, 0)

    return lax.fori_loop(0, listed.shape[0] - UNROLL, step, 0, unroll=8)


def inside(col, low, high):
    return jnp.logical_and(col >= low, col < high)


def fill_blocks(ext, at, parts):
    for part in parts:
        n = part.shape[0] // 128
        ext[pl.ds(at, n)] = part[...].reshape(n, 128, part.shape[1])
        at += n


def early_kernel(late, rows, cols, tiles, *rest):
    parts, (total, ext, listed) = rest[:-3], rest[-3:]
    total[...] = jnp.zeros_like(total)
    low, high = late
    blocks = total.shape[0]
    fill_blocks(ext, 0, parts)

    def wanted(t):
        col = cols[0, t]
        return jnp.logical_or(inside(col, blocks, low), inside(col, high, 2 * blocks))

    def y_of(t):
        col = cols[0, t]
        at = col - blocks - jnp.where(col >= high, high - low, 0)
        return ext[jnp.clip(at, 0, ext.shape[0] - 1)]

    count = list_tiles(wanted, listed)
    gathered_sum(
        count, lambda k: listed[k], lambda t: rows[0, t], lambda t: tiles[t], y_of, total
    )


def early_sum(late, rows, cols, tiles, parts, blocks):
    half = parts[0].shape[1]
    depth = sum(p.shape[0] for p in parts) // 128
    count = tiles.shape[0]
    return pl.pallas_call(
        functools.partial(early_kernel, late),
        out_shape=jax.ShapeDtypeStruct((blocks, 128, half), F32),
        in_specs=[SMEM, SMEM] + [VMEM] * (1 + len(parts)),
        out_specs=VMEM,
        scratch_shapes=[
            pltpu.VMEM((depth, 128, half), F32),
            pltpu.SMEM((count + UNROLL,), jnp.int32),
        ],
        name="early_tiles",
        cost_estimate=LIGHT,
        compiler_params=pltpu.CompilerParams(vmem_limit_bytes=24 << 20),
    )(rows, cols, tiles, *parts)


def late_kernel(
    late, rows, cols, tiles, prev, after, y_mid, total_in, total, ext, listed
):
    total[...] = total_in[...]
    low, high = late
    blocks = total.shape[0]
    size = high - low
    reach = prev.shape[0] // 128
    fill_blocks(ext, 0, (y_mid, prev, after))

    def wanted(t):
        col = cols[0, t]
        return jnp.logical_or(
            inside(col, low, high), jnp.logical_or(col < blocks, col >= 2 * blocks)
        )

    def y_of(t):
        col = cols[0, t]
        at = jnp.where(
            col < blocks,
            size + col - (blocks - reach),
            jnp.where(col >= 2 * blocks, size + reach + col - 2 * blocks, col - low),
        )
        return ext[jnp.clip(at, 0, ext.shape[0] - 1)]

    count = list_tiles(wanted, listed)
    gathered_sum(
        count, lambda k: listed[k], lambda t: rows[0, t], lambda t: tiles[t], y_of, total
    )


def late_sum(late, rows, cols, tiles, prev, after, y_mid, total):
    half = y_mid.shape[1]
    count = tiles.shape[0]
    depth = late[1] - late[0] + (prev.shape[0] + after.shape[0]) // 128
    return pl.pallas_call(
        functools.partial(late_kernel, late),
        out_shape=jax.ShapeDtypeStruct(total.shape, F32),
        in_specs=[SMEM, SMEM] + [VMEM] * 5,
        out_specs=VMEM,
        scratch_shapes=[
            pltpu.VMEM((depth, 128, half), F32),
            pltpu.SMEM((count + UNROLL,), jnp.int32),
        ],
        name="late_tiles",
        cost_estimate=LIGHT,
        compiler_params=pltpu.CompilerParams(vmem_limit_bytes=24 << 20),
    )(rows, cols, tiles, prev, after, y_mid, total)


UNIT_OF_KIND = 0b01111000
PART_AT = (0, 2, 3, 4, 6)


def final_kernel(
    live_ref, hub_rows, panels, hub_tiles, mask, token, total_in, features, bias, *rest
):
    parts = rest[:-5]
    hidden, stats, total, held, sems = rest[-5:]
    copies = []
    for k, (part, at) in enumerate(zip(parts, PART_AT)):
        to = held.at[pl.ds(at, 2)] if len(part.shape) == 3 else held.at[at]
        copies.append(pltpu.make_async_copy(part, to, sems.at[k]))
        copies[-1].start()
    total[...] = total_in[...]
    marks = columns(mask)
    blocks = total.shape[0]
    for copy in copies:
        copy.wait()
    x, yl, z, c = place()
    hubs = 32

    def panel(t):
        p = panels[0, t]
        kx = ((p >> 3) - x) & 3
        holder = (kx >> 1) ^ 1
        odd = (kx & 1) == 1
        slots = [
            jnp.where(odd, 4 + 2 * (holder ^ c) + (holder ^ pc), kx + (pc ^ c)) for pc in range(2)
        ]
        slabs = []
        for dz in range(2):
            delta = 2 * (p & 3) + dz - z
            kind = delta & 3
            offset = ((kind + 2) & 3) - 2
            far = ((delta - offset) >> 2) & 1
            unit = (UNIT_OF_KIND >> (2 * kind)) & 3
            row = unit * 128 + far * 64 + ((p >> 2) & 1) * hubs
            for pc in range(2):
                slabs.append(held[slots[pc], pl.ds(pl.multiple_of(row, hubs), hubs), :])
        return jnp.concatenate(slabs, 0)

    gathered_sum(
        live_ref[0],
        lambda k: k,
        lambda t: hub_rows[0, t],
        lambda t: hub_tiles[t],
        panel,
        total,
    )
    for b in range(blocks):
        at = pl.ds(b * 128, 128)
        v = total[b] + bias[...]
        filled = chosen(features[at, :], marks[:, b : b + 1], token[...])
        h = filled + v / (1.0 + jnp.exp(-v))
        hidden[at, :] = h
        q = h * h
        s = h[:, :128] + h[:, 128:]
        q = q[:, :128] + q[:, 128:]
        stats[pl.ds(b, 1), :] = jnp.sum(s.T, 0, keepdims=True)
        stats[pl.ds(blocks + b, 1), :] = jnp.sum(q.T, 0, keepdims=True)


def final(scalars, arrays, parts):
    total, features = arrays[3], arrays[4]
    blocks, _, half = total.shape
    n = features.shape[0]
    return pl.pallas_call(
        final_kernel,
        out_shape=[
            jax.ShapeDtypeStruct((n, half), F32),
            jax.ShapeDtypeStruct((2 * blocks, 128), F32),
        ],
        in_specs=[SMEM] * len(scalars) + [VMEM] * len(arrays) + [ANY] * len(parts),
        out_specs=[VMEM, VMEM],
        scratch_shapes=[
            pltpu.VMEM((blocks, 128, half), F32),
            pltpu.VMEM((2 * NX,) + parts[1].shape, F32),
            pltpu.SemaphoreType.DMA((len(parts),)),
        ],
        name="final_tiles",
        cost_estimate=LIGHT,
        compiler_params=pltpu.CompilerParams(vmem_limit_bytes=32 << 20),
    )(*scalars, *arrays, *parts)


def norm_kernel(width, hidden, own, other, gain, out):
    blocks = own.shape[0] // 2
    sums = (own[...] + other[...]) / width
    for b in range(blocks):
        mean = jnp.broadcast_to(sums[b : b + 1], (128, 128)).T
        square = jnp.broadcast_to(sums[blocks + b : blocks + b + 1], (128, 128)).T
        scale = lax.rsqrt(square - mean * mean + 1e-05)
        at = pl.ds(b * 128, 128)
        for k in range(hidden.shape[1] // 128):
            lanes = pl.ds(k * 128, 128)
            out[at, lanes] = (hidden[at, lanes] - mean) * scale * gain[:, lanes]


def normalise(hidden, own, other, gain, width):
    def kernel(*refs):
        norm_kernel(width, *refs)

    return pl.pallas_call(
        kernel,
        out_shape=jax.ShapeDtypeStruct(hidden.shape, F32),
        in_specs=[VMEM] * 4,
        out_specs=VMEM,
        name="normalise",
        cost_estimate=LIGHT,
        compiler_params=pltpu.CompilerParams(vmem_limit_bytes=16 << 20),
    )(hidden, own, other, gain[None, :])


def neighbours(first, last):
    doms = NX * NYL * NZ * NC
    prev = lax.ppermute(last, "dom", [(i, i + 1) for i in range(doms - 1)])
    after = lax.ppermute(first, "dom", [(i + 1, i) for i in range(doms - 1)])
    return prev, after


def shards(
    features,
    infill_mask,
    mask_token,
    local_rows,
    local_cols,
    local_tiles,
    hub_ids,
    hub_count,
    hub_rows,
    hub_panels,
    hub_tiles,
    mix_weight,
    mix_bias,
    norm_gain,
):
    rows, half = features.shape
    blocks = rows // 128
    edge = 512
    wide = 640
    inner = wide - edge
    bounds = (((0, wide), (rows - wide, wide)), ((wide, rows - 2 * wide),))
    mask = infill_mask.reshape(blocks, 128)
    swap = lambda v: send(v, lambda x, yl, z, c, f: (x, yl, z, c, 1 - f))

    own_f = hub_rows_of(hub_ids, infill_mask, features, mask_token)
    own_g = swap(own_f)
    other_f = send(own_f, lambda x, yl, z, c, f: (x, 1 - yl, z, c, f))
    other_g = send(own_f, lambda x, yl, z, c, f: (x, 1 - yl, z, c, 1 - f))
    chunks = [
        jnp.concatenate([features[low : low + size] for low, size in ranges], 0)
        for ranges in bounds
    ]
    chunks, own_g, other_f, other_g = lax.optimization_barrier((chunks, own_g, other_f, other_g))
    chunks_g = [swap(v) for v in chunks]

    y_hub, token_y = mix_hub(own_f, own_g, other_f, other_g, mix_weight)
    own = jnp.concatenate([y_hub, send(y_hub, lambda x, yl, z, c, f: (x, yl, z + 4, c, f))], 0)
    units = [own] + [
        send(own, lambda x, yl, z, c, f: (x, yl, z + d, c, f)) for d in (1, -1, 2)
    ]
    line = jnp.concatenate(units, 0)
    sibling = lambda v: send(v, lambda x, yl, z, c, f: (x, yl, z, 1 - c, f))
    across = send(line, lambda x, yl, z, c, f: (x + 2, yl, z, c, f))
    line_s, chunks_g[0], = lax.optimization_barrier((sibling(line), chunks_g[0]))
    pair = jnp.stack([line, line_s], 0)
    beside = send(pair, lambda x, yl, z, c, f: (x + 1 - 2 * c, yl, z, c, f))

    marks = jnp.concatenate(
        [mask[low // 128 : (low + size) // 128] for low, size in bounds[0]], 0
    )
    y_first, y_left, y_right, y_last = mix(
        chunks[0], chunks_g[0], mix_weight, marks, token_y, (edge, inner, inner, edge)
    )
    late = (blocks + wide // 128, 2 * blocks - wide // 128)
    total = early_sum(
        late,
        local_rows,
        local_cols,
        local_tiles[0],
        (y_first, y_left, y_right, y_last),
        blocks,
    )
    across, y_first, y_last, total = lax.optimization_barrier((across, y_first, y_last, total))
    prev, after = neighbours(y_first, y_last)
    (y_mid,) = mix(
        chunks[1],
        chunks_g[1],
        mix_weight,
        mask[wide // 128 : blocks - wide // 128],
        token_y,
        (rows - 2 * wide,),
    )
    beside, y_mid, prev, after = lax.optimization_barrier((beside, y_mid, prev, after))
    parts = (pair, across, sibling(across), beside, sibling(beside))
    total = late_sum(
        late, local_rows, local_cols, local_tiles[0], prev, after, y_mid, total
    )
    hidden, stats = final(
        (hub_count, hub_rows, hub_panels),
        (hub_tiles[0], mask, mask_token[None, :], total, features, mix_bias[None, :]),
        parts,
    )
    return normalise(hidden, stats, swap(stats), norm_gain, half * lax.axis_size("feat"))


def solution(mesh):
    in_specs = (
        P("dom", "feat"),
        P("dom"),
        P("feat"),
        P("dom", None),
        P("dom", None),
        P("dom", None, None, None),
        P("dom"),
        P("dom"),
        P("dom", None),
        P("dom", None),
        P("dom", None, None, None),
        P(None, "feat"),
        P("feat"),
        P("feat"),
    )
    out_specs = P("dom", "feat")
    return jax.shard_map(shards, mesh=mesh, in_specs=in_specs, out_specs=out_specs, check_vma=False)
```
